32 devices in a mesh: fsdp: 8 (over z, x), seq: 4 (over y, core).
Axes of the slice: x: 2, y: 2, z: 4, core: 2. Of those that a mesh axis runs over, the one named last changes fastest.
Arguments:
- tokens: bfloat16 [8, 1536, 1024], P('fsdp', 'seq'), may hold values from -6 to 6
- doc_starts: int32 [8, 1536], P('fsdp', 'seq'), may hold values from 0 to 1, as said below
- qkv_weight: bfloat16 [1024, 3072], P('fsdp'), may hold values from -0.1875 to 0.1875
- query_bias: bfloat16 [1024], P('fsdp'), may hold values from -1.5 to 1.5
- value_bias: bfloat16 [1024], P('fsdp'), may hold values from -0.5 to 0.5
- out_weight: bfloat16 [1024, 1024], P('fsdp'), may hold values from -1.5 to 1.5
- out_bias: bfloat16 [1024], P('fsdp'), may hold values from -1.5 to 1.5
- norm1_gain: bfloat16 [1024], P('fsdp'), may hold values from 0.5 to 1.5
- norm1_shift: bfloat16 [1024], P('fsdp'), may hold values from -1.5 to 1.5
- up_weight: bfloat16 [1024, 4096], P('fsdp'), may hold values from -0.1875 to 0.1875
- up_bias: bfloat16 [4096], P('fsdp'), may hold values from -1.5 to 1.5
- down_weight: bfloat16 [4096, 1024], P('fsdp'), may hold values from -0.09375 to 0.09375
- down_bias: bfloat16 [1024], P('fsdp'), may hold values from -1.5 to 1.5
- norm2_gain: bfloat16 [1024], P('fsdp'), may hold values from 0.5 to 1.5
- norm2_shift: bfloat16 [1024], P('fsdp'), may hold values from -1.5 to 1.5
- cotangent: bfloat16 [8, 1536, 1024], P('fsdp', 'seq'), may hold values from -6 to 6
Outputs:
- layer_out: bfloat16 [8, 1536, 1024], P('fsdp', 'seq')
- input_grad: float32 [8, 1536, 1024], P('fsdp', 'seq')
- qkv_weight_grad: float32 [1024, 3072], P('fsdp')
- query_bias_grad: float32 [1024], P('fsdp')
- value_bias_grad: float32 [1024], P('fsdp')
- out_weight_grad: float32 [1024, 1024], P('fsdp')
- out_bias_grad: float32 [1024], P('fsdp')
- norm1_gain_grad: float32 [1024], P('fsdp')
- norm1_shift_grad: float32 [1024], P('fsdp')
- up_weight_grad: float32 [1024, 4096], P('fsdp')
- up_bias_grad: float32 [4096], P('fsdp')
- down_weight_grad: float32 [4096, 1024], P('fsdp')
- down_bias_grad: float32 [1024], P('fsdp')
- norm2_gain_grad: float32 [1024], P('fsdp')
- norm2_shift_grad: float32 [1024], P('fsdp')
The draws below stay inside these ranges and needn't reach their ends.
Inputs may be any that keep to these rules, and one draw needn't show every extreme that they name: `doc_starts`: each row's first token starts a document; every document has at most 512 tokens, and each row holds at least one document of exactly 512 tokens.
All inputs are finite; a program needn't handle non-finite values.
Results may differ from the reference program's by a relative error of at most 0.014.
The reference program's roundings to bfloat16 on the way count: a program that leaves them out, or rounds other values in their place, can miss the bound.
Values may be sent and summed in bfloat16 or wider, within the bound.
No kernel may reach another device: no remote copies, remote signals or barrier semaphores. Data moves between devices by JAX's collectives and lax.ppermute only.
A program may use at most 192 MiB of HBM per device.

```python
import jax
import jax.numpy as jnp
from jax import lax

D = 1024
H = 16
HD = 64
FF = 4096
QBLOCK = 512
DOC_MOST = 512
ROWS = 8
SEQ_LEN = 1536


def draw_doc_starts(key, part):
    shortest = max(DOC_MOST // 16, 1)
    count = SEQ_LEN // shortest + 2
    key_sizes, key_which = jax.random.split(key)
    sizes = jax.random.randint(key_sizes, (ROWS, count), shortest, DOC_MOST + 1).astype(jnp.int32)
    which = jax.random.randint(key_which, (ROWS, 1), 0, 2).astype(jnp.int32)
    column = jnp.arange(count, dtype=jnp.int32)[None, :]
    sizes = jnp.where(column == which, DOC_MOST, sizes).astype(jnp.int32)
    begins = (jnp.cumsum(sizes, axis=1) - sizes).astype(jnp.int32)
    position = jnp.arange(SEQ_LEN, dtype=jnp.int32)
    hits = (position[None, :, None] == begins[:, None, :]).astype(jnp.int32)
    return jnp.sum(hits, axis=2).astype(jnp.int32)


def spiked(drawn, key, source, target, shards_of, factor):
    owner, partner = [(jnp.arange(drawn.shape[dim]) // (drawn.shape[dim] // shards_of)).reshape([-1 if axis == dim else 1 for axis in range(drawn.ndim)]) for dim in (source, target)]
    chosen = jax.random.permutation(key, shards_of)[partner]
    strong = (owner == chosen) | (owner == (partner + shards_of // 2) % shards_of)
    return jnp.where(strong, factor * drawn, drawn)


def shard_levels(key, shape, cuts, least, top_value):
    loudness, own = 1.0, jax.random.fold_in(key, 6)
    for dim, shards_of in cuts:
        draws = jnp.exp(jax.random.uniform(jax.random.fold_in(own, dim), (shards_of,), jnp.float32, least / len(cuts), top_value / len(cuts)))
        loudness = loudness * jnp.repeat(draws, shape[dim] // shards_of).reshape([-1 if axis == dim else 1 for axis in range(len(shape))])
    return loudness


def gaussian(stream_key, extent, deviation, reach, cuts=(), kind=jnp.bfloat16):
    entries = jax.random.normal(stream_key, extent, jnp.float32) * deviation
    if len(cuts) > 0:
        entries = shard_levels(stream_key, extent, cuts, -0.22, 0.18) * entries
    return jnp.clip(entries, min=-reach, max=reach).astype(kind)


def noise_with(stream_key, dims, scale, reach, cuts, heavy, held_as=jnp.bfloat16):
    values = scale * jax.random.normal(stream_key, dims, jnp.float32)
    if cuts:
        values = values * shard_levels(stream_key, dims, cuts, -0.22, 0.18)
    return jnp.clip(spiked(values, jax.random.fold_in(stream_key, 3), *heavy), -reach, reach).astype(held_as)


def setup_inputs(seed: int = 0) -> dict:
    seeds = jax.random.split(jax.random.key(seed), 17)
    tokens = noise_with(seeds[0], (ROWS, SEQ_LEN, D), 1.0, 6.0, ((0, 8), (1, 4)), (0, 2, 8, 2.0))
    doc_starts = draw_doc_starts(jax.random.fold_in(seeds[16], 71), 0)
    qkv_weight = gaussian(seeds[2], (D, 3 * D), D ** -0.5, 0.1875, ((0, 8),))
    query_bias = gaussian(seeds[3], (D,), 0.3, 1.5, ((0, 8),))
    value_bias = gaussian(seeds[4], (D,), 0.1, 0.5, ((0, 8),))
    out_weight = gaussian(seeds[5], (D, D), (max(D // 64, 4)) ** -0.5, 1.5, ((0, 8),))
    out_bias = gaussian(seeds[6], (D,), 0.3, 1.5, ((0, 8),))
    norm1_gain = jnp.clip(1.0 + 0.1 * jax.random.normal(seeds[7], (D,), jnp.float32), 0.5, 1.5).astype(jnp.bfloat16)
    norm1_shift = gaussian(seeds[8], (D,), 0.3, 1.5, ((0, 8),))
    up_weight = gaussian(seeds[9], (D, FF), D ** -0.5, 0.1875, ((0, 8),))
    up_bias = gaussian(seeds[10], (FF,), 0.3, 1.5, ((0, 8),))
    down_weight = gaussian(seeds[11], (FF, D), FF ** -0.5, 0.09375, ((0, 8),))
    down_bias = gaussian(seeds[12], (D,), 0.3, 1.5, ((0, 8),))
    norm2_gain = jnp.clip(1.0 + 0.1 * jax.random.normal(seeds[13], (D,), jnp.float32), 0.5, 1.5).astype(jnp.bfloat16)
    norm2_shift = gaussian(seeds[14], (D,), 0.3, 1.5, ((0, 8),))
    cotangent = noise_with(seeds[15], (ROWS, SEQ_LEN, D), 1.0, 6.0, ((0, 8), (1, 4)), (0, 2, 8, 2.0))
    return {"tokens": tokens, "doc_starts": doc_starts, "qkv_weight": qkv_weight, "query_bias": query_bias, "value_bias": value_bias, "out_weight": out_weight, "out_bias": out_bias, "norm1_gain": norm1_gain, "norm1_shift": norm1_shift, "up_weight": up_weight, "up_bias": up_bias, "down_weight": down_weight, "down_bias": down_bias, "norm2_gain": norm2_gain, "norm2_shift": norm2_shift, "cotangent": cotangent}


@jax.custom_vjp
def low(v):
    return lax.optimization_barrier(v.astype(jnp.bfloat16)).astype(jnp.float32)

@jax.custom_vjp
def low_back(v):
    return v

def low_keep(v):
    return (low(v), None)

def low_pass(kept, grad):
    return (grad,)

def back_keep(v):
    return (v, None)

def back_low(kept, grad):
    return (low(grad),)
low.defvjp(low_keep, low_pass)
low_back.defvjp(back_keep, back_low)
EPSILON = 1e-05

def product(left, right):
    return jnp.dot(left, right, precision=lax.Precision.HIGHEST)

def layer_norm(hidden, gain, shift):
    center = hidden - lax.optimization_barrier(jnp.mean(hidden, axis=-1, keepdims=True))
    spread = lax.optimization_barrier(jnp.mean(center * center, axis=-1, keepdims=True))
    return center * lax.rsqrt(spread + EPSILON) * gain + shift

def row_attention(query_row, key_row, value_row, segment_row):
    scale = HD ** (-0.5)
    blocks = SEQ_LEN // QBLOCK
    query_blocks = query_row.reshape(blocks, QBLOCK, H, HD)
    segment_blocks = segment_row.reshape(blocks, QBLOCK)

    def one_block(pair):
        query_block, segment_block = pair
        scores = jnp.einsum('qhd,khd->hqk', query_block, key_row, precision=lax.Precision.HIGHEST) * scale
        scores = low_back(scores)
        allowed = (segment_block[:, None] == segment_row[None, :])[None]
        scores = jnp.where(allowed, scores, -jnp.inf)
        weights = low(jax.nn.softmax(scores, axis=-1))
        context = jnp.einsum('hqk,khd->qhd', weights, value_row, precision=lax.Precision.HIGHEST)
        return low(low_back(context))
    return lax.map(jax.checkpoint(one_block), (query_blocks, segment_blocks)).reshape(SEQ_LEN, H * HD)

def per_row(group):
    return row_attention(group[0], group[1], group[2], group[3])

def forward(tokens_f, segment, qkv_weight, query_bias, value_bias, out_weight, out_bias, norm1_gain, norm1_shift, up_weight, up_bias, down_weight, down_bias, norm2_gain, norm2_shift):
    flat = tokens_f.reshape(ROWS * SEQ_LEN, D)
    mixed = product(flat, qkv_weight)
    query = low(low_back(mixed[:, :D] + query_bias))
    key_part = low(low_back(mixed[:, D:2 * D]))
    value_part = low(low_back(mixed[:, 2 * D:] + value_bias))
    shape_four = (ROWS, SEQ_LEN, H, HD)
    context = lax.map(jax.checkpoint(per_row), (query.reshape(shape_four), key_part.reshape(shape_four), value_part.reshape(shape_four), segment))
    context = context.reshape(ROWS * SEQ_LEN, D)
    attended = low_back(product(context, out_weight) + out_bias)
    first = layer_norm(flat + attended, norm1_gain, norm1_shift)
    raised = low_back(product(low(first), up_weight) + up_bias)
    active = low(jax.nn.gelu(raised, approximate=False))
    lowered = low_back(product(active, down_weight) + down_bias)
    return layer_norm(first + lowered, norm2_gain, norm2_shift).reshape(ROWS, SEQ_LEN, D)

def reference(tokens, doc_starts, qkv_weight, query_bias, value_bias, out_weight, out_bias, norm1_gain, norm1_shift, up_weight, up_bias, down_weight, down_bias, norm2_gain, norm2_shift, cotangent):
    segment = jnp.cumsum(doc_starts, axis=1).astype(jnp.int32)
    params = (qkv_weight, query_bias, value_bias, out_weight, out_bias, norm1_gain, norm1_shift, up_weight, up_bias, down_weight, down_bias, norm2_gain, norm2_shift)
    floats = tuple((param.astype(jnp.float32) for param in params))

    def wrapped(tokens_f, *weights):
        return forward(tokens_f, segment, *weights)
    output, pullback = jax.vjp(wrapped, tokens.astype(jnp.float32), *floats)
    grads = pullback(cotangent.astype(jnp.float32))
    return (output.astype(jnp.bfloat16), grads[0], grads[1], grads[2], grads[3], grads[4], grads[5], grads[6], grads[7], grads[8], grads[9], grads[10], grads[11], grads[12], grads[13])
```

```python
import jax
import jax.numpy as jnp
from jax import lax
from jax.sharding import PartitionSpec as P

D = 1024
HD = 64
QBLOCK = 512


EPSILON = 1e-05


def swap(value, bit):
    count = lax.axis_size("seq")
    return lax.ppermute(value, "seq", [(place, place ^ bit) for place in range(count)])


def bits():
    count = lax.axis_size("seq")
    return [1 << power for power in reversed(range(count.bit_length() - 1))]


def gather_row(mine):
    blocks = {0: mine}
    for bit in bits():
        for place in sorted(blocks):
            blocks[place | bit] = swap(blocks[place], bit)
    return [blocks[place] for place in sorted(blocks)]


def sum_row(blocks):
    held = dict(enumerate(blocks))
    for bit in reversed(bits()):
        for place in sorted(held, reverse=True):
            if place & bit:
                term = swap(held.pop(place).astype(jnp.bfloat16), bit)
                held[place ^ bit] = held[place ^ bit] + term.astype(jnp.float32)
    return held[0]


def exchange_row(blocks):
    return [blocks[0]] + [swap(block, place) for place, block in enumerate(blocks) if place]


def in_order(blocks):
    mine, stacked = lax.axis_index("seq"), jnp.stack(blocks)
    return [lax.dynamic_index_in_dim(stacked, mine ^ place, 0, False) for place in range(len(blocks))]


def my_part(value, axis, groups=1):
    count, mine = lax.axis_size("seq"), lax.axis_index("seq")
    group = value.shape[axis] // groups
    width = group // count
    parts = [
        lax.dynamic_slice_in_dim(value, start * group + mine * width, width, axis)
        for start in range(groups)
    ]
    return parts[0] if groups == 1 else jnp.concatenate(parts, axis)


def whole_columns(pieces, groups):
    count, rows, columns = pieces.shape
    width = columns // groups
    return (
        pieces.reshape(count, rows, groups, width)
        .transpose(1, 2, 0, 3)
        .reshape(rows, groups * count * width)
    )


def split_rows(value, count):
    size = value.shape[0] // count
    return [value[place * size : (place + 1) * size] for place in range(count)]


def contract_rows(left, right):
    return lax.dot_general(
        left, right, (((0,), (0,)), ((), ())), preferred_element_type=jnp.float32
    )


def contract_cols(left, right):
    return lax.dot_general(
        left, right, (((1,), (1,)), ((), ())), preferred_element_type=jnp.float32
    )


def exact_gelu(values):
    return jax.nn.gelu(values, approximate=False)


def normalize(hidden, gain, shift):
    center = hidden - jnp.mean(hidden, axis=-1, keepdims=True)
    inverse = lax.rsqrt(jnp.mean(center * center, axis=-1, keepdims=True) + EPSILON)
    normed = center * inverse
    return (normed * gain + shift, normed, inverse)


def norm_back(incoming, normed, inverse, gain):
    scaled = incoming * gain
    d_hidden = inverse * (
        scaled
        - jnp.mean(scaled, axis=-1, keepdims=True)
        - normed * jnp.mean(scaled * normed, axis=-1, keepdims=True)
    )
    return (d_hidden, jnp.sum(incoming * normed, axis=0), jnp.sum(incoming, axis=0))


def masked_scores(query_block, segment_block, key_rows, segment, scale):
    scores = (
        jnp.einsum("qhd,khd->hqk", query_block, key_rows, preferred_element_type=jnp.float32)
        * scale
    )
    allowed = (segment_block[:, None] == segment[None, :])[None]
    return jnp.where(allowed, scores, -jnp.inf)


def attend(head_query, head_key, head_value, segment):
    length = head_query.shape[0]
    heads = head_query.shape[1] // HD
    blocks = length // QBLOCK
    scale = HD ** (-0.5)
    key_rows = head_key.reshape(length, heads, HD)
    value_rows = head_value.reshape(length, heads, HD)
    query_blocks = head_query.reshape(blocks, QBLOCK, heads, HD)
    segment_blocks = segment.reshape(blocks, QBLOCK)

    def one_block(carry, pair):
        query_block, segment_block = pair
        scores = masked_scores(query_block, segment_block, key_rows, segment, scale)
        highest = jnp.max(scores, axis=-1, keepdims=True)
        exponent = jnp.exp(scores - highest)
        total = jnp.sum(exponent, axis=-1, keepdims=True)
        weights = (exponent / total).astype(jnp.bfloat16)
        context = jnp.einsum(
            "hqk,khd->qhd", weights, value_rows, preferred_element_type=jnp.float32
        )
        context = context.astype(jnp.bfloat16).reshape(QBLOCK, heads * HD)
        return (carry, (context, (highest + jnp.log(total))[..., 0]))

    unused, (context, log_total) = lax.scan(one_block, 0, (query_blocks, segment_blocks))
    return (context.reshape(length, heads * HD), log_total)


def attend_back(head_query, head_key, head_value, segment, log_total, head_grad):
    length = head_query.shape[0]
    heads = head_query.shape[1] // HD
    blocks = length // QBLOCK
    scale = HD ** (-0.5)
    key_rows = head_key.reshape(length, heads, HD)
    value_rows = head_value.reshape(length, heads, HD)
    query_blocks = head_query.reshape(blocks, QBLOCK, heads, HD)
    grad_blocks = head_grad.reshape(blocks, QBLOCK, heads, HD)
    segment_blocks = segment.reshape(blocks, QBLOCK)

    def one_block(carry, group):
        sum_key, sum_value = carry
        query_block, segment_block, total_block, grad_block = group
        scores = masked_scores(query_block, segment_block, key_rows, segment, scale)
        probs = jnp.exp(scores - total_block[..., None])
        d_probs = jnp.einsum(
            "qhd,khd->hqk", grad_block, value_rows, preferred_element_type=jnp.float32
        )
        centre = jnp.sum(probs * d_probs, axis=-1, keepdims=True)
        d_scores = (probs * (d_probs - centre)).astype(jnp.bfloat16)
        d_query = (
            jnp.einsum("hqk,khd->qhd", d_scores, key_rows, preferred_element_type=jnp.float32)
            * scale
        )
        sum_key = (
            sum_key
            + jnp.einsum("hqk,qhd->khd", d_scores, query_block, preferred_element_type=jnp.float32)
            * scale
        )
        sum_value = sum_value + jnp.einsum(
            "hqk,qhd->khd",
            probs.astype(jnp.bfloat16),
            grad_block,
            preferred_element_type=jnp.float32,
        )
        return ((sum_key, sum_value), d_query.astype(jnp.bfloat16).reshape(QBLOCK, heads * HD))

    zeros = jnp.zeros((length, heads, HD), jnp.float32)
    (sum_key, sum_value), d_query = lax.scan(
        one_block, (zeros, zeros), (query_blocks, segment_blocks, log_total, grad_blocks)
    )
    return (
        d_query.reshape(length, heads * HD),
        sum_key.reshape(length, heads * HD).astype(jnp.bfloat16),
        sum_value.reshape(length, heads * HD).astype(jnp.bfloat16),
    )


def body(
    tokens,
    doc_starts,
    qkv_weight,
    query_bias,
    value_bias,
    out_weight,
    out_bias,
    norm1_gain,
    norm1_shift,
    up_weight,
    up_bias,
    down_weight,
    down_bias,
    norm2_gain,
    norm2_shift,
    cotangent,
):
    low = jnp.bfloat16
    seq, owners = lax.axis_size("seq"), lax.axis_size("fsdp")
    place, owner = lax.axis_index("seq"), lax.axis_index("fsdp")
    inputs = tokens[0]
    heads_width = D // seq

    w_qkv = lax.all_gather(my_part(qkv_weight, 1, 3), "fsdp", axis=0, tiled=True)
    small = jnp.concatenate(
        [
            query_bias, value_bias, out_bias, norm1_gain, norm1_shift,
            down_bias, norm2_gain, norm2_shift, up_bias,
        ]
    )
    small = lax.all_gather(small, "fsdp")
    each = D // owners
    vectors = [small[:, i * each : (i + 1) * each].reshape(D) for i in range(8)]
    b_query, b_value, b_out, gain_one, shift_one, b_down, gain_two, shift_two = vectors
    b_up = my_part(small[:, 8 * each :], 1).reshape(-1)
    my_up = my_part(up_weight, 1, owners)
    my_down = my_part(down_weight, 0)
    if my_up.shape[0] == my_down.shape[0]:
        joined = jnp.concatenate([out_weight, my_up, my_down], axis=1)
        joined = lax.all_gather(joined, "fsdp", axis=0, tiled=True)
        edge = D + my_up.shape[1]
        w_out, w_up, w_down = joined[:, :D], joined[:, D:edge], joined[:, edge:]
    else:
        w_out = lax.all_gather(out_weight, "fsdp", axis=0, tiled=True)
        w_up = lax.all_gather(my_up, "fsdp", axis=0, tiled=True)
        w_down = lax.all_gather(my_down, "fsdp", axis=0, tiled=True)
    out_rows = [
        lax.dynamic_slice_in_dim(w_out, (place ^ k) * heads_width, heads_width, 0)
        for k in range(seq)
    ]
    w_out = jnp.concatenate(out_rows, axis=0)

    row = jnp.concatenate(gather_row(inputs), axis=0)
    starts = lax.all_gather(doc_starts[0], "seq", axis=0, tiled=True)
    counts = jnp.cumsum(starts).reshape(seq, -1)
    segment = jnp.concatenate(
        [lax.dynamic_index_in_dim(counts, place ^ k, 0, False) for k in range(seq)]
    )

    mixed = jnp.dot(row, w_qkv, preferred_element_type=jnp.float32)
    query = (mixed[:, :heads_width] + my_part(b_query, 0)).astype(low)
    key_part = mixed[:, heads_width : 2 * heads_width].astype(low)
    value_part = (mixed[:, 2 * heads_width :] + my_part(b_value, 0)).astype(low)
    head_context, log_total = attend(query, key_part, value_part, segment)
    context = jnp.concatenate(exchange_row(split_rows(head_context, seq)), axis=1)
    attended = jnp.dot(context, w_out, preferred_element_type=jnp.float32) + b_out
    first, normed_one, inverse_one = normalize(
        inputs.astype(jnp.float32) + attended, gain_one, shift_one
    )
    first_row = gather_row(first.astype(low))
    raised, active, partial = [], [], []
    for block in first_row:
        lifted = jnp.dot(block, w_up, preferred_element_type=jnp.float32) + b_up
        bent = exact_gelu(lifted).astype(low)
        raised.append(lifted)
        active.append(bent)
        partial.append(jnp.dot(bent, w_down, preferred_element_type=jnp.float32))
    lowered = sum_row(partial) + b_down
    result, normed_two, inverse_two = normalize(first + lowered, gain_two, shift_two)

    upstream = cotangent[0].astype(jnp.float32)
    grad_two, d_gain_two, d_shift_two = norm_back(upstream, normed_two, inverse_two, gain_two)
    d_lowered = grad_two.astype(low)
    d_b_down = jnp.sum(d_lowered.astype(jnp.float32), axis=0)
    d_lowered_row = gather_row(d_lowered)
    d_raised, partial = [], []
    for block, lifted in zip(d_lowered_row, raised):
        d_active = contract_cols(block, w_down)
        unused, gelu_back = jax.vjp(exact_gelu, lifted)
        slope = gelu_back(d_active)[0].astype(low)
        d_raised.append(slope)
        partial.append(contract_cols(slope, w_up))
    d_first = sum_row(partial) + grad_two
    d_raised = jnp.concatenate(d_raised, axis=0)
    d_w_down = contract_rows(
        jnp.concatenate(active, axis=0), jnp.concatenate(d_lowered_row, axis=0)
    ).astype(low)
    d_w_up = contract_rows(jnp.concatenate(first_row, axis=0), d_raised).astype(low)
    d_b_up = jnp.sum(d_raised.astype(jnp.float32), axis=0)
    if my_up.shape[0] == my_down.shape[0]:
        pair = jnp.concatenate([d_w_up, d_w_down], axis=1)
        pair = lax.psum_scatter(pair, "fsdp", scatter_dimension=0, tiled=True)
        pair = lax.all_gather(pair, "seq")
        edge = d_w_up.shape[1]
        up_pieces, down_pieces = pair[:, :, :edge], pair[:, :, edge:]
    else:
        up_pieces = lax.psum_scatter(d_w_up, "fsdp", scatter_dimension=0, tiled=True)
        down_pieces = lax.psum_scatter(d_w_down, "fsdp", scatter_dimension=0, tiled=True)
        up_pieces = lax.all_gather(up_pieces, "seq")
        down_pieces = lax.all_gather(down_pieces, "seq")
    up_grad = whole_columns(up_pieces, owners).astype(jnp.float32)
    down_grad = down_pieces.reshape(-1, D).astype(jnp.float32)

    grad_one, d_gain_one, d_shift_one = norm_back(d_first, normed_one, inverse_one, gain_one)
    d_attended = grad_one.astype(low)
    d_b_out = jnp.sum(d_attended.astype(jnp.float32), axis=0)
    d_context = contract_cols(d_attended, w_out).astype(low)
    d_context = [d_context[:, k * heads_width : (k + 1) * heads_width] for k in range(seq)]
    head_grad = jnp.concatenate(exchange_row(d_context), axis=0)
    d_query, d_key, d_value = attend_back(
        query, key_part, value_part, segment, log_total, head_grad
    )
    d_mixed = jnp.concatenate([d_query, d_key, d_value], axis=1)
    d_w_qkv = contract_rows(row, d_mixed).astype(low)
    partial = [contract_cols(block, w_qkv) for block in split_rows(d_mixed, seq)]
    input_grad = grad_one + sum_row(partial)

    d_attended_row = jnp.concatenate(gather_row(d_attended), axis=0)
    d_w_out = contract_rows(head_context, d_attended_row).astype(low)
    columns = [
        lax.dynamic_slice_in_dim(d_w_out, (place ^ k) * heads_width, heads_width, 1)
        for k in range(seq)
    ]
    d_w_out = jnp.concatenate(in_order(exchange_row(columns)), axis=0)
    last = jnp.concatenate([d_w_qkv, d_w_out], axis=1)
    last = lax.psum_scatter(last, "fsdp", scatter_dimension=0, tiled=True)
    last = lax.all_gather(last, "seq")
    edge = 3 * heads_width
    qkv_grad = whole_columns(last[:, :, :edge], 3).astype(jnp.float32)
    out_grad = whole_columns(last[:, :, edge:], 1).astype(jnp.float32)

    def set_mine(part):
        whole = jnp.zeros((part.shape[0], seq, part.shape[1]), jnp.float32)
        return lax.dynamic_update_slice_in_dim(whole, part[:, None], place, 1).reshape(-1)

    d_b_query = set_mine(jnp.sum(d_query.astype(jnp.float32), axis=0)[None])
    d_b_value = set_mine(jnp.sum(d_value.astype(jnp.float32), axis=0)[None])
    d_b_up = set_mine(d_b_up.reshape(owners, -1))
    sums = (
        d_b_query, d_b_value, d_b_out, d_gain_one, d_shift_one,
        d_b_down, d_gain_two, d_shift_two, d_b_up,
    )
    totals = lax.psum(jnp.concatenate(sums), ("fsdp", "seq"))
    vectors = []
    for i, part in enumerate(sums):
        share = part.shape[0] // owners
        vectors.append(lax.dynamic_slice_in_dim(totals, i * D + owner * share, share, 0))
    return (
        result.astype(low)[None],
        input_grad[None],
        qkv_grad,
        vectors[0],
        vectors[1],
        out_grad,
        vectors[2],
        vectors[3],
        vectors[4],
        up_grad,
        vectors[8],
        down_grad,
        vectors[5],
        vectors[6],
        vectors[7],
    )


def solution(mesh):
    in_specs = (
        P("fsdp", "seq", None),
        P("fsdp", "seq"),
        P("fsdp", None),
        P("fsdp"),
        P("fsdp"),
        P("fsdp", None),
        P("fsdp"),
        P("fsdp"),
        P("fsdp"),
        P("fsdp", None),
        P("fsdp"),
        P("fsdp", None),
        P("fsdp"),
        P("fsdp"),
        P("fsdp"),
        P("fsdp", "seq", None),
    )
    out_specs = (
        P("fsdp", "seq", None),
        P("fsdp", "seq", None),
        P("fsdp", None),
        P("fsdp"),
        P("fsdp"),
        P("fsdp", None),
        P("fsdp"),
        P("fsdp"),
        P("fsdp"),
        P("fsdp", None),
        P("fsdp"),
        P("fsdp", None),
        P("fsdp"),
        P("fsdp"),
        P("fsdp"),
    )
    return jax.shard_map(body, mesh=mesh, in_specs=in_specs, out_specs=out_specs, check_vma=False)
```

```python
import jax
import jax.numpy as jnp
from jax import lax
from jax.sharding import PartitionSpec as P

D = 1024
HD = 64
QBLOCK = 512


EPSILON = 1e-05


def swap(value, bit):
    count = lax.axis_size("seq")
    return lax.ppermute(value, "seq", [(place, place ^ bit) for place in range(count)])


def bits():
    count = lax.axis_size("seq")
    return [1 << power for power in reversed(range(count.bit_length() - 1))]


def gather_row(mine):
    blocks = {0: mine}
    for bit in bits():
        for place in sorted(blocks):
            blocks[place | bit] = swap(blocks[place], bit)
    return [blocks[place] for place in sorted(blocks)]


def sum_row(blocks):
    held = dict(enumerate(blocks))
    for bit in reversed(bits()):
        for place in sorted(held, reverse=True):
            if place & bit:
                term = swap(held.pop(place).astype(jnp.bfloat16), bit)
                held[place ^ bit] = held[place ^ bit] + term.astype(jnp.float32)
    return held[0]


def exchange_row(blocks):
    return [blocks[0]] + [swap(block, place) for place, block in enumerate(blocks) if place]


def in_order(blocks):
    mine, stacked = lax.axis_index("seq"), jnp.stack(blocks)
    return [lax.dynamic_index_in_dim(stacked, mine ^ place, 0, False) for place in range(len(blocks))]


def my_part(value, axis, groups=1):
    count, mine = lax.axis_size("seq"), lax.axis_index("seq")
    group = value.shape[axis] // groups
    width = group // count
    parts = [
        lax.dynamic_slice_in_dim(value, start * group + mine * width, width, axis)
        for start in range(groups)
    ]
    return parts[0] if groups == 1 else jnp.concatenate(parts, axis)


def whole_columns(pieces, groups):
    count, rows, columns = pieces.shape
    width = columns // groups
    return (
        pieces.reshape(count, rows, groups, width)
        .transpose(1, 2, 0, 3)
        .reshape(rows, groups * count * width)
    )


def split_rows(value, count):
    size = value.shape[0] // count
    return [value[place * size : (place + 1) * size] for place in range(count)]


def contract_rows(left, right):
    return lax.dot_general(
        left, right, (((0,), (0,)), ((), ())), preferred_element_type=jnp.float32
    )


def contract_cols(left, right):
    return lax.dot_general(
        left, right, (((1,), (1,)), ((), ())), preferred_element_type=jnp.float32
    )


def gelu_and_slope(values):
    phi = 0.5 + 0.5 * lax.erf(values * (0.5**0.5))
    density = jnp.exp(-0.5 * values * values) * ((2.0 * jnp.pi) ** -0.5)
    return values * phi, phi + values * density


def as_columns(vectors, rows):
    padded = [jnp.pad(vector, (0, rows - vector.shape[0])) for vector in vectors]
    return jnp.pad(jnp.stack(padded, axis=1), ((0, 0), (0, -len(vectors) % 128)))


def normalize(hidden, gain, shift):
    center = hidden - jnp.mean(hidden, axis=-1, keepdims=True)
    inverse = lax.rsqrt(jnp.mean(center * center, axis=-1, keepdims=True) + EPSILON)
    normed = center * inverse
    return (normed * gain + shift, normed, inverse)


def norm_back(incoming, normed, inverse, gain):
    scaled = incoming * gain
    d_hidden = inverse * (
        scaled
        - jnp.mean(scaled, axis=-1, keepdims=True)
        - normed * jnp.mean(scaled * normed, axis=-1, keepdims=True)
    )
    return (d_hidden, jnp.sum(incoming * normed, axis=0), jnp.sum(incoming, axis=0))


def masked_scores(query_block, segment_block, key_rows, segment, scale):
    scores = (
        jnp.einsum("qhd,khd->hqk", query_block, key_rows, preferred_element_type=jnp.float32)
        * scale
    )
    allowed = (segment_block[:, None] == segment[None, :])[None]
    return jnp.where(allowed, scores, -jnp.inf)


def attend(head_query, head_key, head_value, segment):
    length = head_query.shape[0]
    heads = head_query.shape[1] // HD
    blocks = length // QBLOCK
    scale = HD ** (-0.5)
    key_rows = head_key.reshape(length, heads, HD)
    value_rows = head_value.reshape(length, heads, HD)
    query_blocks = head_query.reshape(blocks, QBLOCK, heads, HD)
    segment_blocks = segment.reshape(blocks, QBLOCK)

    def one_block(carry, pair):
        query_block, segment_block = pair
        scores = masked_scores(query_block, segment_block, key_rows, segment, scale)
        highest = jnp.max(scores, axis=-1, keepdims=True)
        exponent = jnp.exp(scores - highest)
        total = jnp.sum(exponent, axis=-1, keepdims=True)
        weights = (exponent / total).astype(jnp.bfloat16)
        context = jnp.einsum(
            "hqk,khd->qhd", weights, value_rows, preferred_element_type=jnp.float32
        )
        context = context.astype(jnp.bfloat16).reshape(QBLOCK, heads * HD)
        return (carry, (context, (highest + jnp.log(total))[..., 0]))

    unused, (context, log_total) = lax.scan(one_block, 0, (query_blocks, segment_blocks))
    return (context.reshape(length, heads * HD), log_total)


def attend_back(head_query, head_key, head_value, segment, log_total, head_grad):
    length = head_query.shape[0]
    heads = head_query.shape[1] // HD
    blocks = length // QBLOCK
    scale = HD ** (-0.5)
    key_rows = head_key.reshape(length, heads, HD)
    value_rows = head_value.reshape(length, heads, HD)
    query_blocks = head_query.reshape(blocks, QBLOCK, heads, HD)
    grad_blocks = head_grad.reshape(blocks, QBLOCK, heads, HD)
    segment_blocks = segment.reshape(blocks, QBLOCK)

    def one_block(carry, group):
        sum_key, sum_value = carry
        query_block, segment_block, total_block, grad_block = group
        scores = masked_scores(query_block, segment_block, key_rows, segment, scale)
        probs = jnp.exp(scores - total_block[..., None])
        d_probs = jnp.einsum(
            "qhd,khd->hqk", grad_block, value_rows, preferred_element_type=jnp.float32
        )
        centre = jnp.sum(probs * d_probs, axis=-1, keepdims=True)
        d_scores = (probs * (d_probs - centre)).astype(jnp.bfloat16)
        d_query = (
            jnp.einsum("hqk,khd->qhd", d_scores, key_rows, preferred_element_type=jnp.float32)
            * scale
        )
        sum_key = (
            sum_key
            + jnp.einsum("hqk,qhd->khd", d_scores, query_block, preferred_element_type=jnp.float32)
            * scale
        )
        sum_value = sum_value + jnp.einsum(
            "hqk,qhd->khd",
            probs.astype(jnp.bfloat16),
            grad_block,
            preferred_element_type=jnp.float32,
        )
        return ((sum_key, sum_value), d_query.astype(jnp.bfloat16).reshape(QBLOCK, heads * HD))

    zeros = jnp.zeros((length, heads, HD), jnp.float32)
    (sum_key, sum_value), d_query = lax.scan(
        one_block, (zeros, zeros), (query_blocks, segment_blocks, log_total, grad_blocks)
    )
    return (
        d_query.reshape(length, heads * HD),
        sum_key.reshape(length, heads * HD).astype(jnp.bfloat16),
        sum_value.reshape(length, heads * HD).astype(jnp.bfloat16),
    )


def body(
    tokens,
    doc_starts,
    qkv_weight,
    query_bias,
    value_bias,
    out_weight,
    out_bias,
    norm1_gain,
    norm1_shift,
    up_weight,
    up_bias,
    down_weight,
    down_bias,
    norm2_gain,
    norm2_shift,
    cotangent,
):
    low = jnp.bfloat16
    seq, owners = lax.axis_size("seq"), lax.axis_size("fsdp")
    place = lax.axis_index("seq")
    inputs = tokens[0]
    heads_width = D // seq

    each = D // owners
    columns = as_columns(
        [
            query_bias, value_bias, out_bias, norm1_gain, norm1_shift,
            down_bias, norm2_gain, norm2_shift, my_part(up_bias, 0),
        ],
        each,
    )
    w_qkv = jnp.concatenate([my_part(qkv_weight, 1, 3), columns], axis=1)
    w_qkv = lax.all_gather(w_qkv, "fsdp", axis=0, tiled=True)
    small = w_qkv[:, 3 * heads_width :].T
    w_qkv = w_qkv[:, : 3 * heads_width]
    b_query, b_value, b_out, gain_one, shift_one, b_down, gain_two, shift_two = [
        small[i] for i in range(8)
    ]
    b_up = small[8].reshape(owners, each)[:, : up_bias.shape[0] // seq].reshape(-1)
    my_up = my_part(up_weight, 1, owners)
    my_down = my_part(down_weight, 0)
    if my_up.shape[0] == my_down.shape[0]:
        joined = jnp.concatenate([out_weight, my_up, my_down], axis=1)
        joined = lax.all_gather(joined, "fsdp", axis=0, tiled=True)
        edge = D + my_up.shape[1]
        w_out, w_up, w_down = joined[:, :D], joined[:, D:edge], joined[:, edge:]
    else:
        w_out = lax.all_gather(out_weight, "fsdp", axis=0, tiled=True)
        w_up = lax.all_gather(my_up, "fsdp", axis=0, tiled=True)
        w_down = lax.all_gather(my_down, "fsdp", axis=0, tiled=True)
    out_rows = [
        lax.dynamic_slice_in_dim(w_out, (place ^ k) * heads_width, heads_width, 0)
        for k in range(seq)
    ]
    w_out = jnp.concatenate(out_rows, axis=0)

    row = jnp.concatenate(gather_row(inputs), axis=0)
    counts = jnp.cumsum(jnp.stack(gather_row(doc_starts[0])), axis=1)
    spots = place ^ jnp.arange(seq)
    before = (spots[None, :] < spots[:, None]).astype(jnp.int32)
    counts = counts + jnp.sum(before * counts[:, -1][None, :], axis=1)[:, None]
    segment = counts.reshape(-1)

    mixed = jnp.dot(row, w_qkv, preferred_element_type=jnp.float32)
    query = (mixed[:, :heads_width] + my_part(b_query, 0)).astype(low)
    key_part = mixed[:, heads_width : 2 * heads_width].astype(low)
    value_part = (mixed[:, 2 * heads_width :] + my_part(b_value, 0)).astype(low)
    head_context, log_total = attend(query, key_part, value_part, segment)
    context = jnp.concatenate(exchange_row(split_rows(head_context, seq)), axis=1)
    attended = jnp.dot(context, w_out, preferred_element_type=jnp.float32) + b_out
    first, normed_one, inverse_one = normalize(
        inputs.astype(jnp.float32) + attended, gain_one, shift_one
    )
    first_row = gather_row(first.astype(low))
    slopes, active, partial = [], [], []
    for block in first_row:
        raised = jnp.dot(block, w_up, preferred_element_type=jnp.float32) + b_up
        bent, slope = gelu_and_slope(raised)
        bent = bent.astype(low)
        slopes.append(slope)
        active.append(bent)
        partial.append(jnp.dot(bent, w_down, preferred_element_type=jnp.float32))
    lowered = sum_row(partial) + b_down
    result, normed_two, inverse_two = normalize(first + lowered, gain_two, shift_two)

    upstream = cotangent[0].astype(jnp.float32)
    grad_two, d_gain_two, d_shift_two = norm_back(upstream, normed_two, inverse_two, gain_two)
    d_lowered = grad_two.astype(low)
    d_b_down = jnp.sum(d_lowered.astype(jnp.float32), axis=0)
    d_lowered_row = gather_row(d_lowered)
    d_raised, partial = [], []
    for block, slope in zip(d_lowered_row, slopes):
        turned = (contract_cols(block, w_down) * slope).astype(low)
        d_raised.append(turned)
        partial.append(contract_cols(turned, w_up))
    d_first = sum_row(partial) + grad_two
    d_raised = jnp.concatenate(d_raised, axis=0)
    d_w_down = contract_rows(
        jnp.concatenate(active, axis=0), jnp.concatenate(d_lowered_row, axis=0)
    ).astype(low)
    d_w_up = contract_rows(jnp.concatenate(first_row, axis=0), d_raised).astype(low)
    d_b_up = jnp.sum(d_raised.astype(jnp.float32), axis=0)

    grad_one, d_gain_one, d_shift_one = norm_back(d_first, normed_one, inverse_one, gain_one)
    d_attended = grad_one.astype(low)
    d_b_out = jnp.sum(d_attended.astype(jnp.float32), axis=0)
    d_context = contract_cols(d_attended, w_out).astype(low)
    d_context = [d_context[:, k * heads_width : (k + 1) * heads_width] for k in range(seq)]
    head_grad = jnp.concatenate(exchange_row(d_context), axis=0)
    d_b_up = d_b_up.reshape(owners, -1)
    d_b_up = jnp.pad(d_b_up, ((0, 0), (0, each - d_b_up.shape[1]))).reshape(-1)
    columns = as_columns(
        [d_b_out, d_gain_one, d_shift_one, d_b_down, d_gain_two, d_shift_two, d_b_up], D
    ).astype(low)
    if my_up.shape[0] == my_down.shape[0]:
        pair = jnp.concatenate([d_w_up, d_w_down, columns], axis=1)
        head_grad, pair = lax.optimization_barrier((head_grad, pair))
        pair = lax.psum_scatter(pair, "fsdp", scatter_dimension=0, tiled=True)
        pair = lax.all_gather(pair, "seq")
        edge = d_w_up.shape[1]
        up_pieces, down_pieces = pair[:, :, :edge], pair[:, :, edge : edge + D]
        column_pieces = pair[:, :, edge + D :]
    else:
        up_pieces = jnp.concatenate([d_w_up, columns], axis=1)
        up_pieces = lax.psum_scatter(up_pieces, "fsdp", scatter_dimension=0, tiled=True)
        down_pieces = lax.psum_scatter(d_w_down, "fsdp", scatter_dimension=0, tiled=True)
        up_pieces = lax.all_gather(up_pieces, "seq")
        down_pieces = lax.all_gather(down_pieces, "seq")
        edge = d_w_up.shape[1]
        up_pieces, column_pieces = up_pieces[:, :, :edge], up_pieces[:, :, edge:]
    up_grad = whole_columns(up_pieces, owners).astype(jnp.float32)
    down_grad = down_pieces.reshape(-1, D).astype(jnp.float32)
    small_grads = jnp.sum(column_pieces.astype(jnp.float32), axis=0).T
    up_bias_grad = column_pieces[:, : up_bias.shape[0] // seq, 6].reshape(-1).astype(jnp.float32)
    d_query, d_key, d_value = attend_back(
        query, key_part, value_part, segment, log_total, head_grad
    )
    d_mixed = jnp.concatenate([d_query, d_key, d_value], axis=1)
    d_w_qkv = contract_rows(row, d_mixed).astype(low)
    partial = [contract_cols(block, w_qkv) for block in split_rows(d_mixed, seq)]
    input_grad = grad_one + sum_row(partial)

    d_attended_row = jnp.concatenate(gather_row(d_attended), axis=0)
    d_w_out = contract_rows(head_context, d_attended_row).astype(low)
    columns = [
        lax.dynamic_slice_in_dim(d_w_out, (place ^ k) * heads_width, heads_width, 1)
        for k in range(seq)
    ]
    d_w_out = jnp.concatenate(in_order(exchange_row(columns)), axis=0)

    def set_mine(part):
        whole = jnp.zeros((D,), jnp.float32)
        part = jnp.sum(part.astype(jnp.float32), axis=0)
        return lax.dynamic_update_slice_in_dim(whole, part, place * heads_width, 0)

    columns = as_columns([set_mine(d_query), set_mine(d_value)], D).astype(low)
    last = jnp.concatenate([d_w_qkv, d_w_out, columns], axis=1)
    last = lax.psum_scatter(last, "fsdp", scatter_dimension=0, tiled=True)
    last = lax.all_gather(last, "seq")
    edge = 3 * heads_width
    qkv_grad = whole_columns(last[:, :, :edge], 3).astype(jnp.float32)
    out_grad = whole_columns(last[:, :, edge : edge + heads_width], 1).astype(jnp.float32)
    late_grads = jnp.sum(last[:, :, edge + heads_width :].astype(jnp.float32), axis=0).T
    return (
        result.astype(low)[None],
        input_grad[None],
        qkv_grad,
        late_grads[0],
        late_grads[1],
        out_grad,
        small_grads[0],
        small_grads[1],
        small_grads[2],
        up_grad,
        up_bias_grad,
        down_grad,
        small_grads[3],
        small_grads[4],
        small_grads[5],
    )


def solution(mesh):
    in_specs = (
        P("fsdp", "seq", None),
        P("fsdp", "seq"),
        P("fsdp", None),
        P("fsdp"),
        P("fsdp"),
        P("fsdp", None),
        P("fsdp"),
        P("fsdp"),
        P("fsdp"),
        P("fsdp", None),
        P("fsdp"),
        P("fsdp", None),
        P("fsdp"),
        P("fsdp"),
        P("fsdp"),
        P("fsdp", "seq", None),
    )
    out_specs = (
        P("fsdp", "seq", None),
        P("fsdp", "seq", None),
        P("fsdp", None),
        P("fsdp"),
        P("fsdp"),
        P("fsdp", None),
        P("fsdp"),
        P("fsdp"),
        P("fsdp"),
        P("fsdp", None),
        P("fsdp"),
        P("fsdp", None),
        P("fsdp"),
        P("fsdp"),
        P("fsdp"),
    )
    return jax.shard_map(body, mesh=mesh, in_specs=in_specs, out_specs=out_specs, check_vma=False)
```
